512 devices in a mesh: gx: 64 (over z_lo, y, core), gy: 8 (over x, z_hi).
Axes of the slice: x: 4, y: 8, z: 8 (z_hi: 2, z_lo: 4; z = z_hi * 4 + z_lo), core: 2. Of those that a mesh axis runs over, the one named last changes fastest.
Arguments:
- forward_field: bfloat16 [2560, 128, 128], P('gy', 'gx'), may hold values from -6 to 6
- adjoint_field: bfloat16 [2560, 128, 128], P('gy', 'gx'), may hold values from -6 to 6
- row_scale: float32 [2560, 128], P('gy', 'gx'), may hold values from 0.5 to 2
- station_block: bfloat16 [2560, 2560], P('gy'), may hold values from -0.15625 to 0.15625
- jacobian_block: bfloat16 [2560, 2560], P('gy'), may hold values from -0.15625 to 0.15625
- shock_stations: int32 [16], replicated, may hold values from 0 to 127, as said below
Outputs:
- forward_image: bfloat16 [2560, 128, 128], P('gy', 'gx')
- adjoint_image: bfloat16 [2560, 128, 128], P('gy', 'gx')
The draws below stay inside these ranges and needn't reach their ends.
Inputs may be any that keep to these rules, and one draw needn't show every extreme that they name: `shock_stations`: station indices, repeats possible; station 0 and station 128 - 1 are always listed.
All inputs are finite; a program needn't handle non-finite values.
Results may differ from the reference program's by a relative error of at most 0.013.
Values may be sent and summed in bfloat16 or wider, within the bound.
A program may use at most 64 MiB of HBM per device.

```python
import math
import jax
import jax.numpy as jnp
from jax import lax

NU = 2560
COLS = 128
STATIONS = 128
SHOCKS = 16
N_GY = 8


def draw_shock_stations(key, part):
    picked = jax.random.permutation(key, STATIONS)[:SHOCKS]
    places = jnp.arange(SHOCKS)
    listed = jnp.where(places == 0, 0, jnp.where(places == 1, STATIONS - 1, picked))
    return listed.astype(jnp.int32)


def strengthened(entries, own_key, source, target, blocks, factor):
    def block_of(axis_at):
        return (jnp.arange(entries.shape[axis_at]) // (entries.shape[axis_at] // blocks)).reshape((-1,) + (1,) * (entries.ndim - 1 - axis_at))

    near = jax.random.permutation(own_key, blocks)[block_of(target)]
    other_side = (block_of(target) + blocks // 2) % blocks
    return jnp.where((block_of(source) == near) | (block_of(source) == other_side), factor * entries, entries)


def steps_of(key, shape, shards, low, top_value):
    level = 1.0
    for axis_at, shards_of in shards:
        draws = jax.random.uniform(jax.random.fold_in(jax.random.fold_in(key, 6), axis_at), (shards_of,), jnp.float32, low / len(shards), top_value / len(shards))
        level = level * jnp.repeat(jnp.exp(draws), shape[axis_at] // shards_of).reshape((-1,) + (1,) * (len(shape) - 1 - axis_at))
    return level


def normal_values(stream_key, extent, scale, reach, shards=(), held_as=jnp.bfloat16):
    values = scale * jax.random.normal(stream_key, extent, jnp.float32)
    if shards:
        values = values * steps_of(stream_key, extent, shards, -0.22, 0.18)
    return jnp.clip(values, -reach, reach).astype(held_as)


def heavy_noise(rng, dims, width, limit, shards, heavy, held_as=jnp.bfloat16):
    values = width * jax.random.normal(rng, dims, jnp.float32)
    if shards:
        values = values * steps_of(rng, dims, shards, -0.22, 0.18)
    return jnp.clip(strengthened(values, jax.random.fold_in(rng, 3), *heavy), -limit, limit).astype(held_as)


def setup_inputs(seed: int = 0) -> dict:
    splits = jax.random.split(jax.random.key(seed), 7)
    return {
        "forward_field": normal_values(splits[0], (NU, STATIONS, COLS), 1.0, 6.0, ((0, 8), (1, 64))),
        "adjoint_field": normal_values(splits[1], (NU, STATIONS, COLS), 1.0, 6.0, ((0, 8), (1, 64))),
        "row_scale": jnp.clip(jnp.exp(math.log(2.0) - 1.3862944 * jax.random.uniform(splits[2], (NU, STATIONS), jnp.float32) ** steps_of(splits[2], (NU, STATIONS), ((0, 8), (1, 64)), -0.2, 0.2)), 0.5, 2.0),
        "station_block": heavy_noise(splits[3], (NU, NU), NU ** -0.5, 0.15625, ((0, 8),), (0, 1, 8, 2.0)),
        "jacobian_block": heavy_noise(splits[4], (NU, NU), NU ** -0.5, 0.15625, ((0, 8),), (0, 1, 8, 2.0)),
        "shock_stations": draw_shock_stations(jax.random.fold_in(splits[6], 71), 0),
    }


far_coeff = 1.0 / 12.0
near_coeff = 8.0 / 12.0
shock_gain = 0.5


def streamwise(ext, count):
    values = ext.astype(jnp.float32)
    return ((far_coeff * values[:, 0:count] - near_coeff * values[:, 1:1 + count]) + near_coeff * values[:, 3:3 + count]) - far_coeff * values[:, 4:4 + count]


def transposed(ext, count):
    values = ext.astype(jnp.float32)
    return ((far_coeff * values[:, 4:4 + count] - near_coeff * values[:, 3:3 + count]) + near_coeff * values[:, 1:1 + count]) - far_coeff * values[:, 0:count]


def second_diff(ext, count):
    values = ext.astype(jnp.float32)
    return (values[:, 1:1 + count] - 2.0 * values[:, 2:2 + count]) + values[:, 3:3 + count]


def reference(forward_field, adjoint_field, row_scale, station_block, jacobian_block, shock_stations):
    flat = STATIONS * COLS
    sigma = jnp.any(jnp.arange(STATIONS, dtype=jnp.int32)[:, None] == shock_stations[None, :], axis=1).astype(jnp.float32)
    sigma_ext = jnp.pad(sigma, (2, 2))
    q_ext = jnp.pad(forward_field, ((0, 0), (2, 2), (0, 0)))
    slope = streamwise(q_ext, STATIONS).astype(jnp.bfloat16)
    dense = jnp.dot(station_block, forward_field.reshape(NU, flat), preferred_element_type=jnp.float32)
    flux = jnp.dot(jacobian_block, slope.reshape(NU, flat), preferred_element_type=jnp.float32)
    forward_out = row_scale[:, :, None] * dense.reshape(NU, STATIONS, COLS) + flux.reshape(NU, STATIONS, COLS)
    forward_out = forward_out + shock_gain * sigma[None, :, None] * second_diff(q_ext, STATIONS)
    w_ext = jnp.pad(adjoint_field, ((0, 0), (2, 2), (0, 0)))
    back = transposed(w_ext, STATIONS).astype(jnp.bfloat16).reshape(NU, flat)
    scaled = (row_scale[:, :, None] * adjoint_field.astype(jnp.float32)).astype(jnp.bfloat16).reshape(NU, flat)
    block = NU // N_GY
    total = jnp.zeros((NU, flat), jnp.float32)
    for index in range(N_GY):
        lower = index * block
        part = jnp.dot(station_block[lower:lower + block].T, scaled[lower:lower + block], preferred_element_type=jnp.float32)
        part = part + jnp.dot(jacobian_block[lower:lower + block].T, back[lower:lower + block], preferred_element_type=jnp.float32)
        rounded = lax.optimization_barrier(part.astype(jnp.bfloat16))
        total = total + rounded.astype(jnp.float32)
    weighted = sigma_ext[None, :, None] * w_ext.astype(jnp.float32)
    adjoint_out = total.reshape(NU, STATIONS, COLS) + shock_gain * second_diff(weighted, STATIONS)
    return forward_out.astype(jnp.bfloat16), adjoint_out.astype(jnp.bfloat16)
```

```python
import functools

import jax
import jax.numpy as jnp
from jax import lax
from jax.experimental import pallas as pl
from jax.experimental.pallas import tpu as pltpu
from jax.sharding import PartitionSpec as P

FAR = 1.0 / 12.0
NEAR = 8.0 / 12.0
SHOCK_GAIN = 0.5
N_X = 4
N_Z = 8
N_ZLO = 4
MESH = pl.DeviceIdType.MESH
N_MSG = 40


def kernel(
    n_gx,
    q_ref, w_ref, scale_ref, shock_ref, a_hbm, j_hbm,
    fo_ref, ao_ref,
    aj, qb, tb, sb, facc, wl, wr, zq, rx, acc, zs, zt, rz, pr, pn,
    local_sem, send_sem, recv_sem,
):
    f32, bf16 = jnp.float32, jnp.bfloat16
    rows, flat = q_ref.shape
    half = rows // 2
    width = flat // 2
    inner = n_gx // N_ZLO
    up, lo = pl.ds(0, half), pl.ds(half, half)
    c0, c1 = slice(0, width), slice(width, flat)

    gx, gy = lax.axis_index("gx"), lax.axis_index("gy")
    x, h = gy // 2, gy % 2
    z = h * N_ZLO + gx // inner
    xs = [(x + d) % N_X for d in range(N_X)]

    def at_z(zz):
        return {"gx": (zz % N_ZLO) * inner + gx % inner, "gy": x * 2 + zz // N_ZLO}

    right = {"gx": gx, "gy": xs[1] * 2 + h}
    left = {"gx": gx, "gy": xs[3] * 2 + h}
    z_up, z_dn = at_z((z + 2) % N_Z), at_z((z + N_Z - 2) % N_Z)
    g_next = {"gx": (gx + 1) % n_gx, "gy": gy}
    g_prev = {"gx": (gx + n_gx - 1) % n_gx, "gy": gy}

    started = []

    def message(i, src, dst, dev):
        return pltpu.make_async_remote_copy(
            src_ref=src, dst_ref=dst, send_sem=send_sem.at[i], recv_sem=recv_sem.at[i],
            device_id=dev, device_id_type=MESH,
        )

    def send(i, src, dst, dev):
        copy = message(i, src, dst, dev)
        copy.start()
        started.append(copy)

    def arrived(i, dst, dev):
        message(i, dst, dst, dev).wait_recv()

    load_a = pltpu.make_async_copy(a_hbm, aj.at[pl.ds(0, rows)], local_sem.at[0])
    load_j = pltpu.make_async_copy(j_hbm, aj.at[pl.ds(rows, rows)], local_sem.at[1])
    load_a.start()
    load_j.start()

    barrier = pltpu.get_barrier_semaphore()
    for dev in (right, left, z_up, z_dn, g_next, g_prev):
        pl.semaphore_signal(barrier, inc=1, device_id=dev, device_id_type=MESH)
    pl.semaphore_wait(barrier, 6)

    send(2, q_ref.at[up], zq.at[0], z_up)
    send(3, q_ref.at[lo], zq.at[1], z_dn)
    send(4, q_ref.at[up], qb.at[gy, up], right)
    send(6, q_ref.at[lo], qb.at[gy, lo], left)
    send(0, w_ref, wl, g_next)
    send(1, w_ref, wr, g_prev)
    send(5, q_ref.at[lo], qb.at[gy, lo], right)
    send(7, q_ref.at[up], qb.at[gy, up], left)
    qb[gy] = q_ref[...]

    has_prev = jnp.where(gx > 0, 1.0, 0.0).astype(f32)
    has_next = jnp.where(gx < n_gx - 1, 1.0, 0.0).astype(f32)
    arrived(0, wl, g_prev)
    arrived(1, wr, g_next)
    w0, w1 = w_ref[:, c0].astype(f32), w_ref[:, c1].astype(f32)
    l0, l1 = wl[:, c0].astype(f32) * has_prev, wl[:, c1].astype(f32) * has_prev
    r0, r1 = wr[:, c0].astype(f32) * has_next, wr[:, c1].astype(f32) * has_next
    s0, s1 = scale_ref[:, 0:1], scale_ref[:, 1:2]
    sb[pl.ds(0, rows), c0] = (s0 * w0).astype(bf16)
    sb[pl.ds(0, rows), c1] = (s1 * w1).astype(bf16)
    sb[pl.ds(rows, rows), c0] = (((FAR * r0 - NEAR * w1) + NEAR * l1) - FAR * l0).astype(bf16)
    sb[pl.ds(rows, rows), c1] = (((FAR * r1 - NEAR * r0) + NEAR * w0) - FAR * l1).astype(bf16)
    load_a.wait()
    load_j.wait()

    def columns(d):
        return pl.ds(pl.multiple_of(xs[d] * (2 * rows), 128), 2 * rows)

    def transposed_block(d):
        t = lax.dot_general(
            aj[:, columns(d)], sb[...], (((0,), (0,)), ((), ())), preferred_element_type=f32
        ).astype(bf16)
        tb[2 * d] = t[:rows]
        tb[2 * d + 1] = t[rows:]

    transposed_block(2)
    gl, gr = xs[3] * 2 + h, xs[1] * 2 + h
    arrived(4, qb.at[gl, up], left)
    send(8, qb.at[gl, up], qb.at[gl, up], right)
    arrived(6, qb.at[gr, lo], right)
    send(9, qb.at[gr, lo], qb.at[gr, lo], left)

    def first_far(k, base):
        part = 4 + (1 - h if k == 0 else h)
        send(base, tb.at[part, up], rx.at[k, 0, 0], right)
        send(base + 1, tb.at[part, lo], rx.at[k, 1, 0], left)

    def first_near(k, base):
        hh = 1 - h if k == 0 else h
        send(base + 2, tb.at[2 + hh, lo], rx.at[k, 0, 1], right)
        send(base + 3, tb.at[6 + hh, up], rx.at[k, 1, 1], left)

    def second(k, base):
        hh = 1 - h if k == 0 else h
        arrived(base, rx.at[k, 0, 0], left)
        acc[k, 0] = (tb[2 + hh, up, :].astype(f32) + rx[k, 0, 0].astype(f32)).astype(bf16)
        arrived(base + 1, rx.at[k, 1, 0], right)
        acc[k, 1] = (tb[6 + hh, lo, :].astype(f32) + rx[k, 1, 0].astype(f32)).astype(bf16)
        send(base + 4, acc.at[k, 0], rx.at[k, 0, 2], right)
        send(base + 5, acc.at[k, 1], rx.at[k, 1, 2], left)

    def summed(k, base):
        hh = 1 - h if k == 0 else h
        arrived(base + 2, rx.at[k, 0, 1], left)
        arrived(base + 3, rx.at[k, 1, 1], right)
        arrived(base + 4, rx.at[k, 0, 2], left)
        arrived(base + 5, rx.at[k, 1, 2], right)
        top = (tb[hh, up, :].astype(f32) + rx[k, 0, 2].astype(f32)) + rx[k, 1, 1].astype(f32)
        bottom = (tb[hh, lo, :].astype(f32) + rx[k, 0, 1].astype(f32)) + rx[k, 1, 2].astype(f32)
        return top, bottom

    transposed_block(1)
    first_far(0, 10)
    gp = x * 2 + (1 - h)
    origin_dn = x * 2 + ((z + N_Z - 2) % N_Z) // N_ZLO
    origin_up = x * 2 + ((z + 2) % N_Z) // N_ZLO
    arrived(2, zq.at[0], z_dn)
    send(22, zq.at[0], qb.at[origin_dn, up], z_up)
    arrived(3, zq.at[1], z_up)
    send(23, zq.at[1], qb.at[origin_up, lo], z_dn)
    transposed_block(3)
    first_near(0, 10)
    transposed_block(0)
    second(0, 10)

    arrived(22, qb.at[gp, up], z_dn)
    send(24, qb.at[gp, up], qb.at[gp, up], right)
    send(27, qb.at[gp, up], qb.at[gp, up], left)
    arrived(23, qb.at[gp, lo], z_up)
    send(26, qb.at[gp, lo], qb.at[gp, lo], left)
    send(25, qb.at[gp, lo], qb.at[gp, lo], right)

    top, bottom = summed(0, 10)
    zs[up, :] = top.astype(bf16)
    zs[lo, :] = bottom.astype(bf16)

    def forward_block(d):
        part = jnp.dot(
            aj[:, columns(d)],
            qb[pl.ds(xs[d] * 2, 2)].reshape(2 * rows, flat),
            preferred_element_type=f32,
        )
        facc[...] = part if d == 0 else facc[...] + part

    forward_block(0)
    send(30, zs.at[up], zt.at[0], z_up)
    send(31, zs.at[lo], zt.at[1], z_dn)
    first_far(1, 16)
    first_near(1, 16)

    gl2, gr2 = xs[3] * 2 + (1 - h), xs[1] * 2 + (1 - h)
    arrived(24, qb.at[gl2, up], left)
    send(28, qb.at[gl2, up], qb.at[gl2, up], right)
    arrived(26, qb.at[gr2, lo], right)
    send(29, qb.at[gr2, lo], qb.at[gr2, lo], left)
    second(1, 16)

    arrived(30, zt.at[0], z_dn)
    send(32, zt.at[0], rz.at[up], z_up)
    arrived(31, zt.at[1], z_up)
    send(33, zt.at[1], rz.at[lo], z_dn)

    arrived(5, qb.at[gl, lo], left)
    arrived(25, qb.at[gl2, lo], left)
    forward_block(3)
    arrived(7, qb.at[gr, up], right)
    arrived(27, qb.at[gr2, up], right)
    forward_block(1)
    far_own, far_other = xs[2] * 2 + h, xs[2] * 2 + (1 - h)
    arrived(8, qb.at[far_own, up], left)
    arrived(9, qb.at[far_own, lo], right)
    arrived(28, qb.at[far_other, up], left)
    arrived(29, qb.at[far_other, lo], right)
    forward_block(2)

    def sigma(offset):
        station = gx * 2 + offset
        hit = jnp.where(shock_ref[0] == station, 1.0, 0.0)
        for k in range(1, shock_ref.shape[0]):
            hit = jnp.where(shock_ref[k] == station, 1.0, hit)
        return hit.astype(f32)

    sig = [sigma(o) for o in (-1, 0, 1, 2)]
    q0, q1 = q_ref[:, c0].astype(f32), q_ref[:, c1].astype(f32)
    flux = pl.ds(rows, rows)
    p0, p1 = facc[flux, c0], facc[flux, c1]
    pn[0, :, c0] = ((FAR * p0 - NEAR * p1) + (SHOCK_GAIN * sig[3]) * q1).astype(bf16)
    pn[0, :, c1] = (FAR * p1).astype(bf16)
    pn[1, :, c0] = (-FAR * p0).astype(bf16)
    pn[1, :, c1] = ((NEAR * p0 - FAR * p1) + (SHOCK_GAIN * sig[0]) * q0).astype(bf16)
    send(34, pn.at[0], pr.at[0], g_next)
    send(35, pn.at[1], pr.at[1], g_prev)

    top, bottom = summed(1, 16)
    add0 = SHOCK_GAIN * ((sig[0] * l1 - 2.0 * sig[1] * w0) + sig[2] * w1)
    add1 = SHOCK_GAIN * ((sig[1] * w0 - 2.0 * sig[2] * w1) + sig[3] * r0)
    arrived(32, rz.at[up], z_dn)
    top = top + rz[up, :].astype(f32)
    ao_ref[up, c0] = (top[:, c0] + add0[:half]).astype(bf16)
    ao_ref[up, c1] = (top[:, c1] + add1[:half]).astype(bf16)
    arrived(33, rz.at[lo], z_up)
    bottom = bottom + rz[lo, :].astype(f32)
    ao_ref[lo, c0] = (bottom[:, c0] + add0[half:]).astype(bf16)
    ao_ref[lo, c1] = (bottom[:, c1] + add1[half:]).astype(bf16)

    base0 = s0 * facc[pl.ds(0, rows), c0] + NEAR * p1 + (SHOCK_GAIN * sig[1]) * (q1 - 2.0 * q0)
    base1 = s1 * facc[pl.ds(0, rows), c1] - NEAR * p0 + (SHOCK_GAIN * sig[2]) * (q0 - 2.0 * q1)
    arrived(34, pr.at[0], g_prev)
    arrived(35, pr.at[1], g_next)
    fo_ref[:, c0] = (
        base0 + has_prev * pr[0, :, c0].astype(f32) + has_next * pr[1, :, c0].astype(f32)
    ).astype(bf16)
    fo_ref[:, c1] = (
        base1 + has_prev * pr[0, :, c1].astype(f32) + has_next * pr[1, :, c1].astype(f32)
    ).astype(bf16)

    for copy in started:
        copy.wait_send()


def local(n_gx, q, w, row_scale, station_block, jacobian_block, shock_stations):
    rows, count, width = q.shape
    flat = count * width
    total = station_block.shape[1]
    bf16 = jnp.bfloat16
    vmem = pl.BlockSpec(memory_space=pltpu.VMEM)
    hbm = pl.BlockSpec(memory_space=pl.ANY)
    half = rows // 2
    out = jax.ShapeDtypeStruct((rows, flat), bf16)
    fo, ao = pl.pallas_call(
        functools.partial(kernel, n_gx),
        out_shape=(out, out),
        in_specs=[vmem, vmem, vmem, pl.BlockSpec(memory_space=pltpu.SMEM), hbm, hbm],
        out_specs=(vmem, vmem),
        scratch_shapes=[
            pltpu.VMEM((2 * rows, total), bf16),
            pltpu.VMEM((2 * N_X, rows, flat), bf16),
            pltpu.VMEM((2 * N_X, rows, flat), bf16),
            pltpu.VMEM((2 * rows, flat), bf16),
            pltpu.VMEM((2 * rows, flat), jnp.float32),
            pltpu.VMEM((rows, flat), bf16),
            pltpu.VMEM((rows, flat), bf16),
            pltpu.VMEM((2, half, flat), bf16),
            pltpu.VMEM((2, 2, 3, half, flat), bf16),
            pltpu.VMEM((2, 2, half, flat), bf16),
            pltpu.VMEM((rows, flat), bf16),
            pltpu.VMEM((2, half, flat), bf16),
            pltpu.VMEM((rows, flat), bf16),
            pltpu.VMEM((2, rows, flat), bf16),
            pltpu.VMEM((2, rows, flat), bf16),
            pltpu.SemaphoreType.DMA((2,)),
            pltpu.SemaphoreType.DMA((N_MSG,)),
            pltpu.SemaphoreType.DMA((N_MSG,)),
        ],
        compiler_params=pltpu.CompilerParams(
            collective_id=0, has_side_effects=True, vmem_limit_bytes=40 * 1024 * 1024
        ),
    )(
        q.reshape(rows, flat), w.reshape(rows, flat), row_scale, shock_stations,
        station_block, jacobian_block,
    )
    return fo.reshape(rows, count, width), ao.reshape(rows, count, width)


def solution(mesh):
    in_specs = (
        P("gy", "gx", None),
        P("gy", "gx", None),
        P("gy", "gx"),
        P("gy", None),
        P("gy", None),
        P(),
    )
    out_specs = (P("gy", "gx", None), P("gy", "gx", None))
    return jax.shard_map(
        functools.partial(local, mesh.shape["gx"]),
        mesh=mesh, in_specs=in_specs, out_specs=out_specs, check_vma=False,
    )
```

```python
import functools

import jax
import jax.numpy as jnp
from jax import lax
from jax.experimental import pallas as pl
from jax.experimental.pallas import tpu as pltpu
from jax.sharding import PartitionSpec as P

FAR = 1.0 / 12.0
NEAR = 8.0 / 12.0
SHOCK_GAIN = 0.5
N_X = 4
N_Z = 8
N_ZLO = 4
MESH = pl.DeviceIdType.MESH
N_MSG = 64
N_PIECE = 4


def kernel(
    n_gx,
    q_ref, w_ref, scale_hbm, shock_hbm, a_hbm, j_hbm,
    fo_ref, ao_ref,
    scale_ref, shock_ref, aj, qb, tb, sb, facc, wl, wr, rx, acc, zs, rz, pr, pn,
    local_sem, send_sem, recv_sem,
):
    f32, bf16 = jnp.float32, jnp.bfloat16
    rows, flat = q_ref.shape
    tall = rows // N_PIECE
    width = flat // 2
    span = [pl.ds(p * tall, tall) for p in range(N_PIECE)]
    n_up = N_PIECE // 2
    c0, c1 = slice(0, width), slice(width, flat)

    gx, gy = lax.axis_index("gx"), lax.axis_index("gy")
    x, h = gy // 2, gy % 2
    xs = [(x + d) % N_X for d in range(N_X)]

    right = {"gx": gx, "gy": xs[1] * 2 + h}
    left = {"gx": gx, "gy": xs[3] * 2 + h}
    far = {"gx": gx, "gy": x * 2 + (1 - h)}
    g_next = {"gx": (gx + 1) % n_gx, "gy": gy}
    g_prev = {"gx": (gx + n_gx - 1) % n_gx, "gy": gy}

    started = []

    def message(i, src, dst, dev):
        return pltpu.make_async_remote_copy(
            src_ref=src, dst_ref=dst, send_sem=send_sem.at[i], recv_sem=recv_sem.at[i],
            device_id=dev, device_id_type=MESH,
        )

    def send(i, src, dst, dev):
        copy = message(i, src, dst, dev)
        copy.start()
        started.append(copy)

    def arrived(i, dst, dev):
        message(i, dst, dst, dev).wait_recv()

    load_a = pltpu.make_async_copy(a_hbm, aj.at[pl.ds(0, rows)], local_sem.at[0])
    load_j = pltpu.make_async_copy(j_hbm, aj.at[pl.ds(rows, rows)], local_sem.at[1])
    load_scale = pltpu.make_async_copy(scale_hbm, scale_ref, local_sem.at[2])
    load_shock = pltpu.make_async_copy(shock_hbm, shock_ref, local_sem.at[3])
    load_scale.start()
    load_a.start()
    load_j.start()
    load_shock.start()

    barrier = pltpu.get_barrier_semaphore()
    for dev in (right, left, far, g_next, g_prev):
        pl.semaphore_signal(barrier, inc=1, device_id=dev, device_id_type=MESH)
    pl.semaphore_wait(barrier, 5)

    AG_Z, RS_Z = 4, 8
    AG_OWN, AG_FAR, RS_FAR, RS_OWN = 12, 24, 36, 48
    z_order = [p for i in range(n_up) for p in (i, n_up + i)]

    def spread(base, source, g, pieces):
        for p in pieces:
            send(base + p, source.at[span[p]], qb.at[g, span[p]], right)
        for p in pieces:
            q = (p + n_up) % N_PIECE
            send(base + 4 + q, source.at[span[q]], qb.at[g, span[q]], left)

    def pass_on(base, hh, i):
        gl, gr, j = xs[3] * 2 + hh, xs[1] * 2 + hh, n_up + i
        arrived(base + i, qb.at[gl, span[i]], left)
        send(base + 8 + i, qb.at[gl, span[i]], qb.at[gl, span[i]], right)
        arrived(base + 4 + j, qb.at[gr, span[j]], right)
        send(base + 8 + j, qb.at[gr, span[j]], qb.at[gr, span[j]], left)

    for p in z_order:
        send(AG_Z + p, q_ref.at[span[p]], qb.at[gy, span[p]], far)
    spread(AG_OWN, q_ref, gy, range(n_up))
    send(0, w_ref, wl, g_next)
    send(1, w_ref, wr, g_prev)
    spread(AG_OWN, q_ref, gy, range(n_up, N_PIECE))
    qb[gy] = q_ref[...]

    has_prev = jnp.where(gx > 0, 1.0, 0.0).astype(f32)
    has_next = jnp.where(gx < n_gx - 1, 1.0, 0.0).astype(f32)
    for i in range(n_up):
        pass_on(AG_OWN, h, i)
    arrived(0, wl, g_prev)
    arrived(1, wr, g_next)
    w0, w1 = w_ref[:, c0].astype(f32), w_ref[:, c1].astype(f32)
    l0, l1 = wl[:, c0].astype(f32) * has_prev, wl[:, c1].astype(f32) * has_prev
    r0, r1 = wr[:, c0].astype(f32) * has_next, wr[:, c1].astype(f32) * has_next
    load_scale.wait()
    scale = scale_ref[...].T
    s0, s1 = scale[:, 0:1], scale[:, 1:2]
    sb[pl.ds(0, rows), c0] = (s0 * w0).astype(bf16)
    sb[pl.ds(0, rows), c1] = (s1 * w1).astype(bf16)
    sb[pl.ds(rows, rows), c0] = (((FAR * r0 - NEAR * w1) + NEAR * l1) - FAR * l0).astype(bf16)
    sb[pl.ds(rows, rows), c1] = (((FAR * r1 - NEAR * r0) + NEAR * w0) - FAR * l1).astype(bf16)
    load_a.wait()
    load_j.wait()

    def columns(d):
        return pl.ds(pl.multiple_of(xs[d] * (2 * rows), 128), 2 * rows)

    def transposed_block(d):
        t = lax.dot_general(
            aj[:, columns(d)], sb[...], (((0,), (0,)), ((), ())), preferred_element_type=f32
        ).astype(bf16)
        tb[2 * d] = t[:rows]
        tb[2 * d + 1] = t[rows:]

    def first_far(k, base):
        part = 4 + (1 - h if k == 0 else h)
        for i in range(n_up):
            j = n_up + i
            send(base + i, tb.at[part, span[i]], rx.at[k, 0, 0, i], right)
            send(base + j, tb.at[part, span[j]], rx.at[k, 1, 0, i], left)

    def first_near(k, base):
        hh = 1 - h if k == 0 else h
        for i in range(n_up):
            j = n_up + i
            send(base + 4 + j, tb.at[2 + hh, span[j]], rx.at[k, 0, 1, i], right)
            send(base + 4 + i, tb.at[6 + hh, span[i]], rx.at[k, 1, 1, i], left)

    def second(k, base, i):
        hh = 1 - h if k == 0 else h
        j = n_up + i
        arrived(base + i, rx.at[k, 0, 0, i], left)
        acc[k, i] = (tb[2 + hh, span[i], :].astype(f32) + rx[k, 0, 0, i].astype(f32)).astype(bf16)
        arrived(base + j, rx.at[k, 1, 0, i], right)
        acc[k, j] = (tb[6 + hh, span[j], :].astype(f32) + rx[k, 1, 0, i].astype(f32)).astype(bf16)
        send(base + 8 + i, acc.at[k, i], rx.at[k, 0, 2, i], right)
        send(base + 8 + j, acc.at[k, j], rx.at[k, 1, 2, i], left)

    def summed(k, base, p):
        hh = 1 - h if k == 0 else h
        i = p % n_up
        side = 1 if p < n_up else 0
        arrived(base + 4 + p, rx.at[k, side, 1, i], right if side else left)
        arrived(base + 8 + p, rx.at[k, 1 - side, 2, i], left if side else right)
        return (tb[hh, span[p], :].astype(f32) + rx[k, 1 - side, 2, i].astype(f32)) + rx[
            k, side, 1, i
        ].astype(f32)

    transposed_block(2)
    transposed_block(1)
    first_far(0, RS_FAR)
    transposed_block(3)
    first_near(0, RS_FAR)
    transposed_block(0)

    gp = x * 2 + (1 - h)

    def from_partner(i):
        for p in (i, n_up + i):
            arrived(AG_Z + p, qb.at[gp, span[p]], far)
        spread(AG_FAR, qb.at[gp], gp, [i])
        spread(AG_FAR, qb.at[gp], gp, [n_up + i])

    from_partner(0)
    second(0, RS_FAR, 0)
    second(0, RS_FAR, 1)
    from_partner(1)
    for p in z_order:
        zs[span[p], :] = summed(0, RS_FAR, p).astype(bf16)
        send(RS_Z + p, zs.at[span[p]], rz.at[span[p]], far)

    def forward_block(d):
        part = jnp.dot(
            aj[:, columns(d)],
            qb[pl.ds(xs[d] * 2, 2)].reshape(2 * rows, flat),
            preferred_element_type=f32,
        )
        facc[...] = part if d == 0 else facc[...] + part

    for i in range(n_up):
        pass_on(AG_FAR, 1 - h, i)
    first_far(1, RS_OWN)
    first_near(1, RS_OWN)
    forward_block(0)

    def whole_from(d, dev, base):
        for hh, first in ((h, AG_OWN), (1 - h, AG_FAR)):
            for p in range(N_PIECE):
                done = (p < n_up) == (base == 0)
                if not done:
                    arrived(first + base + p, qb.at[xs[d] * 2 + hh, span[p]], dev)
        forward_block(d)

    whole_from(3, left, 0)
    whole_from(1, right, 4)
    for hh, first in ((h, AG_OWN), (1 - h, AG_FAR)):
        for p in range(N_PIECE):
            arrived(first + 8 + p, qb.at[xs[2] * 2 + hh, span[p]], left if p < n_up else right)
    forward_block(2)

    def sigma(offset):
        station = gx * 2 + offset
        hit = jnp.where(shock_ref[0] == station, 1.0, 0.0)
        for k in range(1, shock_ref.shape[0]):
            hit = jnp.where(shock_ref[k] == station, 1.0, hit)
        return hit.astype(f32)

    load_shock.wait()
    sig = [sigma(o) for o in (-1, 0, 1, 2)]
    q0, q1 = q_ref[:, c0].astype(f32), q_ref[:, c1].astype(f32)
    flux = pl.ds(rows, rows)
    p0, p1 = facc[flux, c0], facc[flux, c1]
    pn[0, :, c0] = ((FAR * p0 - NEAR * p1) + (SHOCK_GAIN * sig[3]) * q1).astype(bf16)
    pn[0, :, c1] = (FAR * p1).astype(bf16)
    pn[1, :, c0] = (-FAR * p0).astype(bf16)
    pn[1, :, c1] = ((NEAR * p0 - FAR * p1) + (SHOCK_GAIN * sig[0]) * q0).astype(bf16)
    send(2, pn.at[0], pr.at[0], g_next)
    send(3, pn.at[1], pr.at[1], g_prev)

    second(1, RS_OWN, 0)
    second(1, RS_OWN, 1)
    add0 = SHOCK_GAIN * ((sig[0] * l1 - 2.0 * sig[1] * w0) + sig[2] * w1)
    add1 = SHOCK_GAIN * ((sig[1] * w0 - 2.0 * sig[2] * w1) + sig[3] * r0)
    for p in z_order:
        term = summed(1, RS_OWN, p)
        arrived(RS_Z + p, rz.at[span[p]], far)
        term = term + rz[span[p], :].astype(f32)
        own = slice(p * tall, (p + 1) * tall)
        ao_ref[span[p], c0] = (term[:, c0] + add0[own]).astype(bf16)
        ao_ref[span[p], c1] = (term[:, c1] + add1[own]).astype(bf16)

    base0 = s0 * facc[pl.ds(0, rows), c0] + NEAR * p1 + (SHOCK_GAIN * sig[1]) * (q1 - 2.0 * q0)
    base1 = s1 * facc[pl.ds(0, rows), c1] - NEAR * p0 + (SHOCK_GAIN * sig[2]) * (q0 - 2.0 * q1)
    arrived(2, pr.at[0], g_prev)
    arrived(3, pr.at[1], g_next)
    fo_ref[:, c0] = (
        base0 + has_prev * pr[0, :, c0].astype(f32) + has_next * pr[1, :, c0].astype(f32)
    ).astype(bf16)
    fo_ref[:, c1] = (
        base1 + has_prev * pr[0, :, c1].astype(f32) + has_next * pr[1, :, c1].astype(f32)
    ).astype(bf16)

    for copy in started:
        copy.wait_send()


def local(n_gx, q, w, row_scale, station_block, jacobian_block, shock_stations):
    rows, count, width = q.shape
    flat = count * width
    total = station_block.shape[1]
    bf16 = jnp.bfloat16
    vmem = pl.BlockSpec(memory_space=pltpu.VMEM)
    hbm = pl.BlockSpec(memory_space=pltpu.HBM)
    tall = rows // N_PIECE
    out = jax.ShapeDtypeStruct((rows, flat), bf16)
    fo, ao = pl.pallas_call(
        functools.partial(kernel, n_gx),
        out_shape=(out, out),
        in_specs=[vmem, vmem, hbm, hbm, hbm, hbm],
        out_specs=(vmem, vmem),
        scratch_shapes=[
            pltpu.VMEM((count, rows), jnp.float32),
            pltpu.SMEM(shock_stations.shape, jnp.int32),
            pltpu.VMEM((2 * rows, total), bf16),
            pltpu.VMEM((2 * N_X, rows, flat), bf16),
            pltpu.VMEM((2 * N_X, rows, flat), bf16),
            pltpu.VMEM((2 * rows, flat), bf16),
            pltpu.VMEM((2 * rows, flat), jnp.float32),
            pltpu.VMEM((rows, flat), bf16),
            pltpu.VMEM((rows, flat), bf16),
            pltpu.VMEM((2, 2, 3, N_PIECE // 2, tall, flat), bf16),
            pltpu.VMEM((2, N_PIECE, tall, flat), bf16),
            pltpu.VMEM((rows, flat), bf16),
            pltpu.VMEM((rows, flat), bf16),
            pltpu.VMEM((2, rows, flat), bf16),
            pltpu.VMEM((2, rows, flat), bf16),
            pltpu.SemaphoreType.DMA((4,)),
            pltpu.SemaphoreType.DMA((N_MSG,)),
            pltpu.SemaphoreType.DMA((N_MSG,)),
        ],
        compiler_params=pltpu.CompilerParams(
            collective_id=0, has_side_effects=True, vmem_limit_bytes=63 * 1024 * 1024
        ),
    )(
        q.reshape(rows, flat), w.reshape(rows, flat), row_scale.T, shock_stations,
        station_block, jacobian_block,
    )
    return fo.reshape(rows, count, width), ao.reshape(rows, count, width)


def solution(mesh):
    in_specs = (
        P("gy", "gx", None),
        P("gy", "gx", None),
        P("gy", "gx"),
        P("gy", None),
        P("gy", None),
        P(),
    )
    out_specs = (P("gy", "gx", None), P("gy", "gx", None))
    return jax.shard_map(
        functools.partial(local, mesh.shape["gx"]),
        mesh=mesh, in_specs=in_specs, out_specs=out_specs, check_vma=False,
    )
```

```python
import functools

import jax
import jax.numpy as jnp
from jax import lax
from jax.experimental import pallas as pl
from jax.experimental.pallas import tpu as pltpu
from jax.sharding import PartitionSpec as P

FAR = 1.0 / 12.0
NEAR = 8.0 / 12.0
SHOCK_GAIN = 0.5
N_X = 4
N_Z = 8
N_ZLO = 4
MESH = pl.DeviceIdType.MESH
N_MSG = 64
N_PIECE = 4


def kernel(
    n_gx,
    q_ref, w_ref, scale_hbm, shock_hbm, a_hbm, j_hbm,
    fo_ref, ao_ref,
    scale_ref, shock_ref, aj, qb, tb, sb, facc, wl, wr, rx, acc, zs, rz, pr, pn,
    local_sem, send_sem, recv_sem,
):
    f32, bf16 = jnp.float32, jnp.bfloat16
    rows, flat = q_ref.shape
    tall = rows // N_PIECE
    width = flat // 2
    span = [pl.ds(p * tall, tall) for p in range(N_PIECE)]
    n_up = N_PIECE // 2
    c0, c1 = slice(0, width), slice(width, flat)

    gx, gy = lax.axis_index("gx"), lax.axis_index("gy")
    x, h = gy // 2, gy % 2
    xs = [(x + d) % N_X for d in range(N_X)]

    right = {"gx": gx, "gy": xs[1] * 2 + h}
    left = {"gx": gx, "gy": xs[3] * 2 + h}
    far = {"gx": gx, "gy": x * 2 + (1 - h)}
    g_next = {"gx": (gx + 1) % n_gx, "gy": gy}
    g_prev = {"gx": (gx + n_gx - 1) % n_gx, "gy": gy}

    started = []

    def message(i, src, dst, dev):
        return pltpu.make_async_remote_copy(
            src_ref=src, dst_ref=dst, send_sem=send_sem.at[i], recv_sem=recv_sem.at[i],
            device_id=dev, device_id_type=MESH,
        )

    def send(i, src, dst, dev):
        copy = message(i, src, dst, dev)
        copy.start()
        started.append(copy)

    def arrived(i, dst, dev):
        message(i, dst, dst, dev).wait_recv()

    load_a = pltpu.make_async_copy(a_hbm, aj.at[pl.ds(0, rows)], local_sem.at[0])
    load_j = pltpu.make_async_copy(j_hbm, aj.at[pl.ds(rows, rows)], local_sem.at[1])
    load_scale = pltpu.make_async_copy(scale_hbm, scale_ref, local_sem.at[2])
    load_shock = pltpu.make_async_copy(shock_hbm, shock_ref, local_sem.at[3])
    load_scale.start()
    load_a.start()
    load_j.start()
    load_shock.start()

    barrier = pltpu.get_barrier_semaphore()
    for dev in (right, left, far, g_next, g_prev):
        pl.semaphore_signal(barrier, inc=1, device_id=dev, device_id_type=MESH)
    pl.semaphore_wait(barrier, 5)

    AG_Z, RS_Z = 4, 8
    AG_OWN, AG_FAR, RS_FAR, RS_OWN = 12, 24, 36, 48
    z_order = [p for i in range(n_up) for p in (i, n_up + i)]

    def spread(base, source, g, pieces):
        for p in pieces:
            send(base + p, source.at[span[p]], qb.at[g, span[p]], right)
        for p in pieces:
            q = (p + n_up) % N_PIECE
            send(base + 4 + q, source.at[span[q]], qb.at[g, span[q]], left)

    def pass_on(base, hh, i):
        gl, gr, j = xs[3] * 2 + hh, xs[1] * 2 + hh, n_up + i
        arrived(base + i, qb.at[gl, span[i]], left)
        send(base + 8 + i, qb.at[gl, span[i]], qb.at[gl, span[i]], right)
        arrived(base + 4 + j, qb.at[gr, span[j]], right)
        send(base + 8 + j, qb.at[gr, span[j]], qb.at[gr, span[j]], left)

    for p in z_order:
        send(AG_Z + p, q_ref.at[span[p]], qb.at[gy, span[p]], far)
    spread(AG_OWN, q_ref, gy, range(n_up))
    send(0, w_ref, wl, g_next)
    send(1, w_ref, wr, g_prev)
    spread(AG_OWN, q_ref, gy, range(n_up, N_PIECE))
    qb[gy] = q_ref[...]

    has_prev = jnp.where(gx > 0, 1.0, 0.0).astype(f32)
    has_next = jnp.where(gx < n_gx - 1, 1.0, 0.0).astype(f32)
    for i in range(n_up):
        pass_on(AG_OWN, h, i)
    arrived(0, wl, g_prev)
    arrived(1, wr, g_next)
    w0, w1 = w_ref[:, c0].astype(f32), w_ref[:, c1].astype(f32)
    l0, l1 = wl[:, c0].astype(f32) * has_prev, wl[:, c1].astype(f32) * has_prev
    r0, r1 = wr[:, c0].astype(f32) * has_next, wr[:, c1].astype(f32) * has_next
    load_scale.wait()
    scale = scale_ref[...].T
    s0, s1 = scale[:, 0:1], scale[:, 1:2]
    sb[pl.ds(0, rows), c0] = (s0 * w0).astype(bf16)
    sb[pl.ds(0, rows), c1] = (s1 * w1).astype(bf16)
    sb[pl.ds(rows, rows), c0] = (((FAR * r0 - NEAR * w1) + NEAR * l1) - FAR * l0).astype(bf16)
    sb[pl.ds(rows, rows), c1] = (((FAR * r1 - NEAR * r0) + NEAR * w0) - FAR * l1).astype(bf16)
    load_a.wait()
    load_j.wait()

    def columns(d):
        return pl.ds(pl.multiple_of(xs[d] * (2 * rows), 128), 2 * rows)

    def transposed_block(d):
        t = lax.dot_general(
            aj[:, columns(d)], sb[...], (((0,), (0,)), ((), ())), preferred_element_type=f32
        ).astype(bf16)
        tb[2 * d] = t[:rows]
        tb[2 * d + 1] = t[rows:]

    def first_far(k, base):
        part = 4 + (1 - h if k == 0 else h)
        for i in range(n_up):
            j = n_up + i
            send(base + i, tb.at[part, span[i]], rx.at[k, 0, 0, i], right)
            send(base + j, tb.at[part, span[j]], rx.at[k, 1, 0, i], left)

    def first_near(k, base):
        hh = 1 - h if k == 0 else h
        for i in range(n_up):
            j = n_up + i
            send(base + 4 + j, tb.at[2 + hh, span[j]], rx.at[k, 0, 1, i], right)
            send(base + 4 + i, tb.at[6 + hh, span[i]], rx.at[k, 1, 1, i], left)

    def second(k, base, i):
        hh = 1 - h if k == 0 else h
        j = n_up + i
        arrived(base + i, rx.at[k, 0, 0, i], left)
        acc[k, i] = (tb[2 + hh, span[i], :].astype(f32) + rx[k, 0, 0, i].astype(f32)).astype(bf16)
        arrived(base + j, rx.at[k, 1, 0, i], right)
        acc[k, j] = (tb[6 + hh, span[j], :].astype(f32) + rx[k, 1, 0, i].astype(f32)).astype(bf16)
        send(base + 8 + i, acc.at[k, i], rx.at[k, 0, 2, i], right)
        send(base + 8 + j, acc.at[k, j], rx.at[k, 1, 2, i], left)

    def summed(k, base, p):
        hh = 1 - h if k == 0 else h
        i = p % n_up
        side = 1 if p < n_up else 0
        arrived(base + 4 + p, rx.at[k, side, 1, i], right if side else left)
        arrived(base + 8 + p, rx.at[k, 1 - side, 2, i], left if side else right)
        return (tb[hh, span[p], :].astype(f32) + rx[k, 1 - side, 2, i].astype(f32)) + rx[
            k, side, 1, i
        ].astype(f32)

    transposed_block(2)
    transposed_block(1)
    first_far(0, RS_FAR)
    transposed_block(3)
    first_near(0, RS_FAR)
    transposed_block(0)

    gp = x * 2 + (1 - h)

    def from_partner(i):
        for p in (i, n_up + i):
            arrived(AG_Z + p, qb.at[gp, span[p]], far)
        spread(AG_FAR, qb.at[gp], gp, [i])
        spread(AG_FAR, qb.at[gp], gp, [n_up + i])

    from_partner(0)
    second(0, RS_FAR, 0)
    second(0, RS_FAR, 1)
    from_partner(1)
    for p in z_order:
        zs[span[p], :] = summed(0, RS_FAR, p).astype(bf16)
        send(RS_Z + p, zs.at[span[p]], rz.at[span[p]], far)

    def forward_block(d):
        part = jnp.dot(
            aj[:, columns(d)],
            qb[pl.ds(xs[d] * 2, 2)].reshape(2 * rows, flat),
            preferred_element_type=f32,
        )
        facc[...] = part if d == 0 else facc[...] + part

    for i in range(n_up):
        pass_on(AG_FAR, 1 - h, i)
    first_far(1, RS_OWN)
    first_near(1, RS_OWN)
    forward_block(0)

    def whole_from(d, dev, base):
        for hh, first in ((h, AG_OWN), (1 - h, AG_FAR)):
            for p in range(N_PIECE):
                done = (p < n_up) == (base == 0)
                if not done:
                    arrived(first + base + p, qb.at[xs[d] * 2 + hh, span[p]], dev)
        forward_block(d)

    whole_from(3, left, 0)
    whole_from(1, right, 4)
    for hh, first in ((h, AG_OWN), (1 - h, AG_FAR)):
        for p in range(N_PIECE):
            arrived(first + 8 + p, qb.at[xs[2] * 2 + hh, span[p]], left if p < n_up else right)
    forward_block(2)

    def sigma(offset):
        station = gx * 2 + offset
        hit = jnp.where(shock_ref[0] == station, 1.0, 0.0)
        for k in range(1, shock_ref.shape[0]):
            hit = jnp.where(shock_ref[k] == station, 1.0, hit)
        return hit.astype(f32)

    load_shock.wait()
    sig = [sigma(o) for o in (-1, 0, 1, 2)]
    q0, q1 = q_ref[:, c0].astype(f32), q_ref[:, c1].astype(f32)
    flux = pl.ds(rows, rows)
    p0, p1 = facc[flux, c0], facc[flux, c1]
    pn[0, :, c0] = ((FAR * p0 - NEAR * p1) + (SHOCK_GAIN * sig[3]) * q1).astype(bf16)
    pn[0, :, c1] = (FAR * p1).astype(bf16)
    pn[1, :, c0] = (-FAR * p0).astype(bf16)
    pn[1, :, c1] = ((NEAR * p0 - FAR * p1) + (SHOCK_GAIN * sig[0]) * q0).astype(bf16)
    send(2, pn.at[0], pr.at[0], g_next)
    send(3, pn.at[1], pr.at[1], g_prev)

    second(1, RS_OWN, 0)
    second(1, RS_OWN, 1)
    add0 = SHOCK_GAIN * ((sig[0] * l1 - 2.0 * sig[1] * w0) + sig[2] * w1)
    add1 = SHOCK_GAIN * ((sig[1] * w0 - 2.0 * sig[2] * w1) + sig[3] * r0)
    for p in z_order:
        term = summed(1, RS_OWN, p)
        arrived(RS_Z + p, rz.at[span[p]], far)
        term = term + rz[span[p], :].astype(f32)
        own = slice(p * tall, (p + 1) * tall)
        ao_ref[span[p], c0] = (term[:, c0] + add0[own]).astype(bf16)
        ao_ref[span[p], c1] = (term[:, c1] + add1[own]).astype(bf16)

    base0 = s0 * facc[pl.ds(0, rows), c0] + NEAR * p1 + (SHOCK_GAIN * sig[1]) * (q1 - 2.0 * q0)
    base1 = s1 * facc[pl.ds(0, rows), c1] - NEAR * p0 + (SHOCK_GAIN * sig[2]) * (q0 - 2.0 * q1)
    arrived(2, pr.at[0], g_prev)
    arrived(3, pr.at[1], g_next)
    fo_ref[:, c0] = (
        base0 + has_prev * pr[0, :, c0].astype(f32) + has_next * pr[1, :, c0].astype(f32)
    ).astype(bf16)
    fo_ref[:, c1] = (
        base1 + has_prev * pr[0, :, c1].astype(f32) + has_next * pr[1, :, c1].astype(f32)
    ).astype(bf16)

    for copy in started:
        copy.wait_send()


def local(n_gx, q, w, row_scale, station_block, jacobian_block, shock_stations):
    rows, count, width = q.shape
    flat = count * width
    total = station_block.shape[1]
    bf16 = jnp.bfloat16
    vmem = pl.BlockSpec(memory_space=pltpu.VMEM)
    hbm = pl.BlockSpec(memory_space=pltpu.HBM)
    tall = rows // N_PIECE
    out = jax.ShapeDtypeStruct((rows, flat), bf16)
    fo, ao = pl.pallas_call(
        functools.partial(kernel, n_gx),
        out_shape=(out, out),
        in_specs=[vmem, vmem, hbm, hbm, hbm, hbm],
        out_specs=(vmem, vmem),
        scratch_shapes=[
            pltpu.VMEM((count, rows), jnp.float32),
            pltpu.SMEM(shock_stations.shape, jnp.int32),
            pltpu.VMEM((2 * rows, total), bf16),
            pltpu.VMEM((2 * N_X, rows, flat), bf16),
            pltpu.VMEM((2 * N_X, rows, flat), bf16),
            pltpu.VMEM((2 * rows, flat), bf16),
            pltpu.VMEM((2 * rows, flat), jnp.float32),
            pltpu.VMEM((rows, flat), bf16),
            pltpu.VMEM((rows, flat), bf16),
            pltpu.VMEM((2, 2, 3, N_PIECE // 2, tall, flat), bf16),
            pltpu.VMEM((2, N_PIECE, tall, flat), bf16),
            pltpu.VMEM((rows, flat), bf16),
            pltpu.VMEM((rows, flat), bf16),
            pltpu.VMEM((2, rows, flat), bf16),
            pltpu.VMEM((2, rows, flat), bf16),
            pltpu.SemaphoreType.DMA((4,)),
            pltpu.SemaphoreType.DMA((N_MSG,)),
            pltpu.SemaphoreType.DMA((N_MSG,)),
        ],
        compiler_params=pltpu.CompilerParams(
            collective_id=0, has_side_effects=True, vmem_limit_bytes=40 * 1024 * 1024
        ),
    )(
        q.reshape(rows, flat), w.reshape(rows, flat),
        *(pltpu.with_memory_space_constraint(v, pltpu.HBM)
          for v in (row_scale.T, shock_stations, station_block, jacobian_block)),
    )
    return fo.reshape(rows, count, width), ao.reshape(rows, count, width)


def solution(mesh):
    in_specs = (
        P("gy", "gx", None),
        P("gy", "gx", None),
        P("gy", "gx"),
        P("gy", None),
        P("gy", None),
        P(),
    )
    out_specs = (P("gy", "gx", None), P("gy", "gx", None))
    return jax.shard_map(
        functools.partial(local, mesh.shape["gx"]),
        mesh=mesh, in_specs=in_specs, out_specs=out_specs, check_vma=False,
    )
```

```python
import functools

import jax
import jax.numpy as jnp
from jax import lax
from jax.experimental import pallas as pl
from jax.experimental.pallas import tpu as pltpu
from jax.sharding import PartitionSpec as P

FAR = 1.0 / 12.0
NEAR = 8.0 / 12.0
SHOCK_GAIN = 0.5
N_X = 4
N_Z = 8
N_ZLO = 4
MESH = pl.DeviceIdType.MESH
N_MSG = 64
N_PIECE = 4


def kernel(
    n_gx,
    q_ref, w_ref, scale_hbm, shock_hbm, a_hbm, j_hbm,
    fo_ref, ao_ref,
    scale_ref, shock_ref, aj, qb, tb, sb, facc, wl, wr, rx, acc, zs, rz, pr, pn,
    local_sem, send_sem, recv_sem,
):
    f32, bf16 = jnp.float32, jnp.bfloat16
    rows, flat = q_ref.shape
    tall = rows // N_PIECE
    width = flat // 2
    span = [pl.ds(p * tall, tall) for p in range(N_PIECE)]
    n_up = N_PIECE // 2
    c0, c1 = slice(0, width), slice(width, flat)

    gx, gy = lax.axis_index("gx"), lax.axis_index("gy")
    x, h = gy // 2, gy % 2
    xs = [(x + d) % N_X for d in range(N_X)]

    right = {"gx": gx, "gy": xs[1] * 2 + h}
    left = {"gx": gx, "gy": xs[3] * 2 + h}
    far = {"gx": gx, "gy": x * 2 + (1 - h)}
    g_next = {"gx": (gx + 1) % n_gx, "gy": gy}
    g_prev = {"gx": (gx + n_gx - 1) % n_gx, "gy": gy}

    started = []
    first, last = gx == 0, gx == n_gx - 1
    inner_prev, inner_next = jnp.logical_not(first), jnp.logical_not(last)

    def message(i, src, dst, dev):
        return pltpu.make_async_remote_copy(
            src_ref=src, dst_ref=dst, send_sem=send_sem.at[i], recv_sem=recv_sem.at[i],
            device_id=dev, device_id_type=MESH,
        )

    def send(i, src, dst, dev):
        copy = message(i, src, dst, dev)
        copy.start()
        started.append(copy)

    def send_along(there, i, src, dst, dev):
        @pl.when(there)
        def _():
            message(i, src, dst, dev).start()

    def arrived_along(there, i, dst, dev):
        @pl.when(there)
        def _():
            message(i, dst, dst, dev).wait_recv()

    def arrived(i, dst, dev):
        message(i, dst, dst, dev).wait_recv()

    load_a = pltpu.make_async_copy(a_hbm, aj.at[pl.ds(0, rows)], local_sem.at[0])
    load_j = pltpu.make_async_copy(j_hbm, aj.at[pl.ds(rows, rows)], local_sem.at[1])
    load_scale = pltpu.make_async_copy(scale_hbm, scale_ref, local_sem.at[2])
    load_shock = pltpu.make_async_copy(shock_hbm, shock_ref, local_sem.at[3])
    load_scale.start()
    load_a.start()
    load_j.start()
    load_shock.start()

    barrier = pltpu.get_barrier_semaphore()
    for dev in (right, left, far):
        pl.semaphore_signal(barrier, inc=1, device_id=dev, device_id_type=MESH)
    for there, dev in ((inner_prev, g_prev), (inner_next, g_next)):
        @pl.when(there)
        def _(dev=dev):
            pl.semaphore_signal(barrier, inc=1, device_id=dev, device_id_type=MESH)
    inside = jnp.logical_and(inner_prev, inner_next)

    @pl.when(inside)
    def _():
        pl.semaphore_wait(barrier, 5)

    @pl.when(jnp.logical_not(inside))
    def _():
        pl.semaphore_wait(barrier, 4)

    AG_Z, RS_Z = 4, 8
    AG_OWN, AG_FAR, RS_FAR, RS_OWN = 12, 24, 36, 48
    z_order = [p for i in range(n_up) for p in (i, n_up + i)]

    def spread(base, source, g, pieces):
        for p in pieces:
            send(base + p, source.at[span[p]], qb.at[g, span[p]], right)
        for p in pieces:
            q = (p + n_up) % N_PIECE
            send(base + 4 + q, source.at[span[q]], qb.at[g, span[q]], left)

    def pass_on(base, hh, i):
        gl, gr, j = xs[3] * 2 + hh, xs[1] * 2 + hh, n_up + i
        arrived(base + i, qb.at[gl, span[i]], left)
        send(base + 8 + i, qb.at[gl, span[i]], qb.at[gl, span[i]], right)
        arrived(base + 4 + j, qb.at[gr, span[j]], right)
        send(base + 8 + j, qb.at[gr, span[j]], qb.at[gr, span[j]], left)

    for p in z_order:
        send(AG_Z + p, q_ref.at[span[p]], qb.at[gy, span[p]], far)
    spread(AG_OWN, q_ref, gy, range(n_up))
    send_along(inner_next, 0, w_ref, wl, g_next)
    send_along(inner_prev, 1, w_ref, wr, g_prev)
    spread(AG_OWN, q_ref, gy, range(n_up, N_PIECE))
    qb[gy] = q_ref[...]

    @pl.when(first)
    def _():
        wl[...] = jnp.zeros_like(wl)
        pr[0] = jnp.zeros(pr.shape[1:], bf16)

    @pl.when(last)
    def _():
        wr[...] = jnp.zeros_like(wr)
        pr[1] = jnp.zeros(pr.shape[1:], bf16)


    for i in range(n_up):
        pass_on(AG_OWN, h, i)
    arrived_along(inner_prev, 0, wl, g_prev)
    arrived_along(inner_next, 1, wr, g_next)
    w0, w1 = w_ref[:, c0].astype(f32), w_ref[:, c1].astype(f32)
    l0, l1 = wl[:, c0].astype(f32), wl[:, c1].astype(f32)
    r0, r1 = wr[:, c0].astype(f32), wr[:, c1].astype(f32)
    load_scale.wait()
    scale = scale_ref[...].T
    s0, s1 = scale[:, 0:1], scale[:, 1:2]
    sb[pl.ds(0, rows), c0] = (s0 * w0).astype(bf16)
    sb[pl.ds(0, rows), c1] = (s1 * w1).astype(bf16)
    sb[pl.ds(rows, rows), c0] = (((FAR * r0 - NEAR * w1) + NEAR * l1) - FAR * l0).astype(bf16)
    sb[pl.ds(rows, rows), c1] = (((FAR * r1 - NEAR * r0) + NEAR * w0) - FAR * l1).astype(bf16)
    load_a.wait()
    load_j.wait()

    def columns(d):
        return pl.ds(pl.multiple_of(xs[d] * (2 * rows), 128), 2 * rows)

    def transposed_block(d):
        t = lax.dot_general(
            aj[:, columns(d)], sb[...], (((0,), (0,)), ((), ())), preferred_element_type=f32
        ).astype(bf16)
        tb[2 * d] = t[:rows]
        tb[2 * d + 1] = t[rows:]

    def first_far(k, base):
        part = 4 + (1 - h if k == 0 else h)
        for i in range(n_up):
            j = n_up + i
            send(base + i, tb.at[part, span[i]], rx.at[k, 0, 0, i], right)
            send(base + j, tb.at[part, span[j]], rx.at[k, 1, 0, i], left)

    def first_near(k, base):
        hh = 1 - h if k == 0 else h
        for i in range(n_up):
            j = n_up + i
            send(base + 4 + j, tb.at[2 + hh, span[j]], rx.at[k, 0, 1, i], right)
            send(base + 4 + i, tb.at[6 + hh, span[i]], rx.at[k, 1, 1, i], left)

    def second(k, base, i):
        hh = 1 - h if k == 0 else h
        j = n_up + i
        arrived(base + i, rx.at[k, 0, 0, i], left)
        acc[k, i] = (tb[2 + hh, span[i], :].astype(f32) + rx[k, 0, 0, i].astype(f32)).astype(bf16)
        arrived(base + j, rx.at[k, 1, 0, i], right)
        acc[k, j] = (tb[6 + hh, span[j], :].astype(f32) + rx[k, 1, 0, i].astype(f32)).astype(bf16)
        send(base + 8 + i, acc.at[k, i], rx.at[k, 0, 2, i], right)
        send(base + 8 + j, acc.at[k, j], rx.at[k, 1, 2, i], left)

    def summed(k, base, p):
        hh = 1 - h if k == 0 else h
        i = p % n_up
        side = 1 if p < n_up else 0
        arrived(base + 4 + p, rx.at[k, side, 1, i], right if side else left)
        arrived(base + 8 + p, rx.at[k, 1 - side, 2, i], left if side else right)
        return (tb[hh, span[p], :].astype(f32) + rx[k, 1 - side, 2, i].astype(f32)) + rx[
            k, side, 1, i
        ].astype(f32)

    transposed_block(2)
    transposed_block(1)
    first_far(0, RS_FAR)
    transposed_block(3)
    first_near(0, RS_FAR)
    transposed_block(0)

    gp = x * 2 + (1 - h)

    def from_partner(i):
        for p in (i, n_up + i):
            arrived(AG_Z + p, qb.at[gp, span[p]], far)
        spread(AG_FAR, qb.at[gp], gp, [i])
        spread(AG_FAR, qb.at[gp], gp, [n_up + i])

    def forward_block(d):
        part = jnp.dot(
            aj[:, columns(d)],
            qb[pl.ds(xs[d] * 2, 2)].reshape(2 * rows, flat),
            preferred_element_type=f32,
        )
        facc[...] = part if d == 0 else facc[...] + part

    def reduced(i):
        for p in (i, n_up + i):
            zs[span[p], :] = summed(0, RS_FAR, p).astype(bf16)
            send(RS_Z + p, zs.at[span[p]], rz.at[span[p]], far)

    second(0, RS_FAR, 0)
    from_partner(0)
    second(0, RS_FAR, 1)
    from_partner(1)
    reduced(0)
    pass_on(AG_FAR, 1 - h, 0)
    reduced(1)
    pass_on(AG_FAR, 1 - h, 1)
    first_far(1, RS_OWN)
    first_near(1, RS_OWN)
    forward_block(0)

    def whole_from(d, dev, base):
        for hh, first in ((h, AG_OWN), (1 - h, AG_FAR)):
            for p in range(N_PIECE):
                done = (p < n_up) == (base == 0)
                if not done:
                    arrived(first + base + p, qb.at[xs[d] * 2 + hh, span[p]], dev)
        forward_block(d)

    whole_from(3, left, 0)
    whole_from(1, right, 4)
    for hh, first in ((h, AG_OWN), (1 - h, AG_FAR)):
        for p in range(N_PIECE):
            arrived(first + 8 + p, qb.at[xs[2] * 2 + hh, span[p]], left if p < n_up else right)
    forward_block(2)

    def sigma(offset):
        station = gx * 2 + offset
        hit = jnp.where(shock_ref[0] == station, 1.0, 0.0)
        for k in range(1, shock_ref.shape[0]):
            hit = jnp.where(shock_ref[k] == station, 1.0, hit)
        return hit.astype(f32)

    load_shock.wait()
    sig = [sigma(o) for o in (-1, 0, 1, 2)]
    q0, q1 = q_ref[:, c0].astype(f32), q_ref[:, c1].astype(f32)
    flux = pl.ds(rows, rows)
    p0, p1 = facc[flux, c0], facc[flux, c1]
    pn[0, :, c0] = ((FAR * p0 - NEAR * p1) + (SHOCK_GAIN * sig[3]) * q1).astype(bf16)
    pn[0, :, c1] = (FAR * p1).astype(bf16)
    pn[1, :, c0] = (-FAR * p0).astype(bf16)
    pn[1, :, c1] = ((NEAR * p0 - FAR * p1) + (SHOCK_GAIN * sig[0]) * q0).astype(bf16)
    send_along(inner_next, 2, pn.at[0], pr.at[0], g_next)
    send_along(inner_prev, 3, pn.at[1], pr.at[1], g_prev)

    second(1, RS_OWN, 0)
    second(1, RS_OWN, 1)
    add0 = SHOCK_GAIN * ((sig[0] * l1 - 2.0 * sig[1] * w0) + sig[2] * w1)
    add1 = SHOCK_GAIN * ((sig[1] * w0 - 2.0 * sig[2] * w1) + sig[3] * r0)
    for p in z_order:
        term = summed(1, RS_OWN, p)
        arrived(RS_Z + p, rz.at[span[p]], far)
        term = term + rz[span[p], :].astype(f32)
        own = slice(p * tall, (p + 1) * tall)
        ao_ref[span[p], c0] = (term[:, c0] + add0[own]).astype(bf16)
        ao_ref[span[p], c1] = (term[:, c1] + add1[own]).astype(bf16)

    base0 = s0 * facc[pl.ds(0, rows), c0] + NEAR * p1 + (SHOCK_GAIN * sig[1]) * (q1 - 2.0 * q0)
    base1 = s1 * facc[pl.ds(0, rows), c1] - NEAR * p0 + (SHOCK_GAIN * sig[2]) * (q0 - 2.0 * q1)
    arrived_along(inner_prev, 2, pr.at[0], g_prev)
    arrived_along(inner_next, 3, pr.at[1], g_next)
    fo_ref[:, c0] = (
        base0 + pr[0, :, c0].astype(f32) + pr[1, :, c0].astype(f32)
    ).astype(bf16)
    fo_ref[:, c1] = (
        base1 + pr[0, :, c1].astype(f32) + pr[1, :, c1].astype(f32)
    ).astype(bf16)

    for copy in started:
        copy.wait_send()
    for there, i, src, dev in (
        (inner_next, 0, w_ref, g_next), (inner_prev, 1, w_ref, g_prev),
        (inner_next, 2, pn.at[0], g_next), (inner_prev, 3, pn.at[1], g_prev),
    ):
        @pl.when(there)
        def _(i=i, src=src, dev=dev):
            message(i, src, src, dev).wait_send()


def local(n_gx, q, w, row_scale, station_block, jacobian_block, shock_stations):
    rows, count, width = q.shape
    flat = count * width
    total = station_block.shape[1]
    bf16 = jnp.bfloat16
    vmem = pl.BlockSpec(memory_space=pltpu.VMEM)
    hbm = pl.BlockSpec(memory_space=pltpu.HBM)
    tall = rows // N_PIECE
    out = jax.ShapeDtypeStruct((rows, flat), bf16)
    fo, ao = pl.pallas_call(
        functools.partial(kernel, n_gx),
        out_shape=(out, out),
        in_specs=[vmem, vmem, hbm, hbm, hbm, hbm],
        out_specs=(vmem, vmem),
        scratch_shapes=[
            pltpu.VMEM((count, rows), jnp.float32),
            pltpu.SMEM(shock_stations.shape, jnp.int32),
            pltpu.VMEM((2 * rows, total), bf16),
            pltpu.VMEM((2 * N_X, rows, flat), bf16),
            pltpu.VMEM((2 * N_X, rows, flat), bf16),
            pltpu.VMEM((2 * rows, flat), bf16),
            pltpu.VMEM((2 * rows, flat), jnp.float32),
            pltpu.VMEM((rows, flat), bf16),
            pltpu.VMEM((rows, flat), bf16),
            pltpu.VMEM((2, 2, 3, N_PIECE // 2, tall, flat), bf16),
            pltpu.VMEM((2, N_PIECE, tall, flat), bf16),
            pltpu.VMEM((rows, flat), bf16),
            pltpu.VMEM((rows, flat), bf16),
            pltpu.VMEM((2, rows, flat), bf16),
            pltpu.VMEM((2, rows, flat), bf16),
            pltpu.SemaphoreType.DMA((4,)),
            pltpu.SemaphoreType.DMA((N_MSG,)),
            pltpu.SemaphoreType.DMA((N_MSG,)),
        ],
        compiler_params=pltpu.CompilerParams(
            collective_id=0, has_side_effects=True, vmem_limit_bytes=40 * 1024 * 1024
        ),
    )(
        q.reshape(rows, flat), w.reshape(rows, flat),
        *(pltpu.with_memory_space_constraint(v, pltpu.HBM)
          for v in (row_scale.T, shock_stations, station_block, jacobian_block)),
    )
    return fo.reshape(rows, count, width), ao.reshape(rows, count, width)


def solution(mesh):
    in_specs = (
        P("gy", "gx", None),
        P("gy", "gx", None),
        P("gy", "gx"),
        P("gy", None),
        P("gy", None),
        P(),
    )
    out_specs = (P("gy", "gx", None), P("gy", "gx", None))
    return jax.shard_map(
        functools.partial(local, mesh.shape["gx"]),
        mesh=mesh, in_specs=in_specs, out_specs=out_specs, check_vma=False,
    )
```
